32 devices in a mesh: rx: 4 (over z), ry: 8 (over y, x, core).
Axes of the slice: x: 2, y: 2, z: 4, core: 2. Of those that a mesh axis runs over, the one named last changes fastest.
Arguments:
- features: bfloat16 [256, 64, 512], P(('rx', 'ry')), may hold values from -6 to 6
- grad_out: bfloat16 [256, 64, 512], P(('rx', 'ry')), may hold values from -6 to 6
- weights: bfloat16 [27, 64, 64], replicated, may hold values from -0.15625 to 0.15625
- live_count: int32 [32], P(('rx', 'ry')), may hold values from 0 to 8, as said below
- neighbor: int32 [256, 6], P(('rx', 'ry')), may hold values from -1 to 23, as said below
- send_list: int32 [128, 4], P(('rx', 'ry')), may hold values from -1 to 7, as said below
Outputs:
- output: bfloat16 [256, 64, 512], P(('rx', 'ry'))
- grad_features: bfloat16 [256, 64, 512], P(('rx', 'ry'))
- grad_weights: float32 [27, 64, 64], replicated
The draws below stay inside these ranges and needn't reach their ends.
Inputs may be any that keep to these rules, and one draw needn't show every extreme that they name: A device's occupied bricks take its first live_count slots; some device is full. `neighbor`: only live slots have entries other than -1. Entries of 8 or more stand only in columns 0 to 3, equal 8 + s * 4 + k in column s, and never point beyond the grid of devices. Sides 4 and 5 are always within the device. Adjacency is mutual: a brick is its neighbour's neighbour on the opposite side, and each received face slot of a side is used by at most one brick. `send_list`: row 4 d + t lists distinct live slots of device d, their face t going to the device beside d on side t; used entries come first, then -1.
All inputs are finite; a program needn't handle non-finite values.
Results may differ from the reference program's by a relative error of at most 0.0025.
Values may be sent and summed in bfloat16 or wider, within the bound.
A program may use at most 64 MiB of HBM per device.

```python
import jax
import jax.numpy as jnp
from jax import lax

C = 64
RB = 2
H = 2
B_DEV = 8
CAP = 4
BRICKS = 256
N_RX = 4
N_RY = 8


def shift_low(values, axis):
    first = jnp.zeros_like(lax_take(values, axis, 0, 1))
    rest = lax_take(values, axis, 0, values.shape[axis] - 1)
    return jnp.concatenate([first, rest], axis=axis)


def shift_high(values, axis):
    last = jnp.zeros_like(lax_take(values, axis, 0, 1))
    rest = lax_take(values, axis, 1, values.shape[axis] - 1)
    return jnp.concatenate([rest, last], axis=axis)


def lax_take(values, axis, start, length):
    return jnp.take(values, jnp.arange(start, start + length), axis=axis)


def local_value(occupied, slot_rank):
    return jnp.where(occupied == 1, slot_rank, -1)


def pair_keys(pairs):
    shape = pairs.shape
    flat_pairs = pairs.reshape(shape[0], shape[1], -1)
    return (jnp.cumsum(flat_pairs, axis=-1) - 1).reshape(shape).astype(jnp.int32)


def build_bricks(key):
    subkeys = jax.random.split(jax.random.fold_in(key, 4242), 4)
    positions = RB * RB * H
    devices = N_RX * N_RY
    fill_rate = jax.random.randint(subkeys[0], (N_RX, N_RY), 40, 101)
    full_row = jax.random.randint(subkeys[1], (), 0, N_RX - 1)
    full_col = jax.random.randint(subkeys[2], (), 0, N_RY - 1)
    grid_rows = jnp.arange(N_RX)[:, None]
    grid_cols = jnp.arange(N_RY)[None, :]
    full = (grid_rows == full_row) & (grid_cols == full_col) | (grid_rows == full_row + 1) & (grid_cols == full_col) | (grid_rows == full_row) & (grid_cols == full_col + 1)
    fill_rate = jnp.where(full, 101, fill_rate)
    rolls = jax.random.randint(subkeys[3], (N_RX, N_RY, RB, RB, H), 0, 100)
    occupied = (rolls < fill_rate[:, :, None, None, None]).astype(jnp.int32)
    flat_occ = occupied.reshape(N_RX, N_RY, positions)
    slot_rank = (jnp.cumsum(flat_occ, axis=-1) - 1).reshape(occupied.shape).astype(jnp.int32)
    count = flat_occ.sum(-1).reshape(devices).astype(jnp.int32)
    pair_x = occupied[:-1, :, RB - 1] * occupied[1:, :, 0]
    key_x = pair_keys(pair_x)
    pad_x = jnp.zeros((1, N_RY, RB, H), jnp.int32)
    pair_x_low = jnp.concatenate([pad_x, pair_x], 0)
    key_x_low = jnp.concatenate([pad_x, key_x], 0)
    pair_x_high = jnp.concatenate([pair_x, pad_x], 0)
    key_x_high = jnp.concatenate([key_x, pad_x], 0)
    pair_y = occupied[:, :-1, :, RB - 1] * occupied[:, 1:, :, 0]
    key_y = pair_keys(pair_y)
    pad_y = jnp.zeros((N_RX, 1, RB, H), jnp.int32)
    pair_y_low = jnp.concatenate([pad_y, pair_y], 1)
    key_y_low = jnp.concatenate([pad_y, key_y], 1)
    pair_y_high = jnp.concatenate([pair_y, pad_y], 1)
    key_y_high = jnp.concatenate([key_y, pad_y], 1)
    index_x = jnp.arange(RB)[:, None, None]
    index_y = jnp.arange(RB)[None, :, None]
    side_zero = jnp.where(index_x > 0, local_value(shift_low(occupied, 2), shift_low(slot_rank, 2)), jnp.where(pair_x_low[:, :, None] == 1, positions + key_x_low[:, :, None], -1))
    side_one = jnp.where(index_x < RB - 1, local_value(shift_high(occupied, 2), shift_high(slot_rank, 2)), jnp.where(pair_x_high[:, :, None] == 1, positions + CAP + key_x_high[:, :, None], -1))
    side_two = jnp.where(index_y > 0, local_value(shift_low(occupied, 3), shift_low(slot_rank, 3)), jnp.where(pair_y_low[:, :, :, None] == 1, positions + 2 * CAP + key_y_low[:, :, :, None], -1))
    side_three = jnp.where(index_y < RB - 1, local_value(shift_high(occupied, 3), shift_high(slot_rank, 3)), jnp.where(pair_y_high[:, :, :, None] == 1, positions + 3 * CAP + key_y_high[:, :, :, None], -1))
    side_four = local_value(shift_low(occupied, 4), shift_low(slot_rank, 4))
    side_five = local_value(shift_high(occupied, 4), shift_high(slot_rank, 4))
    sides = jnp.stack([side_zero, side_one, side_two, side_three, side_four, side_five], axis=-1)
    sides = jnp.where(occupied[..., None] == 1, sides, -1).astype(jnp.int32)
    slot_of = jnp.where(occupied == 1, slot_rank, positions).reshape(devices, positions)
    device_ids = jnp.broadcast_to(jnp.arange(devices)[:, None], (devices, positions))
    table = jnp.full((devices, positions + 1, 6), -1, jnp.int32)
    table = table.at[device_ids, slot_of].set(sides.reshape(devices, positions, 6))
    neighbor = table[:, :positions].reshape(devices * positions, 6)

    def sender(pairs, keys, slots):
        target = jnp.where(pairs == 1, keys, CAP).reshape(devices, -1)
        owners = jnp.broadcast_to(jnp.arange(devices)[:, None], target.shape)
        listed = jnp.full((devices, CAP + 1), -1, jnp.int32)
        listed = listed.at[owners, target].set(slots.reshape(devices, -1).astype(jnp.int32))
        return listed[:, :CAP]
    send_zero = sender(pair_x_low, key_x_low, slot_rank[:, :, 0])
    send_one = sender(pair_x_high, key_x_high, slot_rank[:, :, RB - 1])
    send_two = sender(pair_y_low, key_y_low, slot_rank[:, :, :, 0])
    send_three = sender(pair_y_high, key_y_high, slot_rank[:, :, :, RB - 1])
    send_list = jnp.stack([send_zero, send_one, send_two, send_three], axis=1).reshape(devices * 4, CAP)
    return (count, neighbor, send_list)


def draw_live_count(key, part):
    return build_bricks(key)[0]


def draw_neighbor(key, part):
    return build_bricks(key)[1]


def draw_send_list(key, part):
    return build_bricks(key)[2]


def level_of(stream_key, dims, cuts, smallest, high):
    def one(position, shards_of):
        steps = jax.random.uniform(jax.random.fold_in(jax.random.fold_in(stream_key, 6), position), (shards_of,), jnp.float32, smallest / len(cuts), high / len(cuts))
        return jnp.repeat(jnp.exp(steps), dims[position] // shards_of).reshape((-1,) + (1,) * (len(dims) - position - 1))

    level = one(*cuts[0])
    for cut in cuts[1:]:
        level = level * one(*cut)
    return level


def gaussian(rng, shape, width, limit, shards=(), held_as=jnp.bfloat16):
    level = level_of(rng, shape, shards, -0.22, 0.18) if shards else 1.0
    values = jax.random.normal(rng, shape, jnp.float32) * width * level
    return jnp.minimum(jnp.maximum(values, -limit), limit).astype(held_as)


def setup_inputs(seed: int = 0) -> dict:
    arg_keys = jax.random.split(jax.random.key(seed), 7)
    return {
        "features": gaussian(arg_keys[0], (BRICKS, C, 512), 1.0, 6.0, ((0, 32),)),
        "grad_out": gaussian(arg_keys[1], (BRICKS, C, 512), 1.0, 6.0, ((0, 32),)),
        "weights": gaussian(arg_keys[2], (27, C, C), (27 * C) ** -0.5, 0.15625),
        "live_count": draw_live_count(jax.random.fold_in(arg_keys[6], 71), 0),
        "neighbor": draw_neighbor(jax.random.fold_in(arg_keys[6], 71), 0),
        "send_list": draw_send_list(jax.random.fold_in(arg_keys[6], 71), 0),
    }


def face_of(cube, s):
    n, c = (cube.shape[0], cube.shape[1])
    if s == 0:
        layer = cube[:, :, 0]
    elif s == 1:
        layer = cube[:, :, 7]
    elif s == 2:
        layer = cube[:, :, :, 0]
    elif s == 3:
        layer = cube[:, :, :, 7]
    elif s == 4:
        layer = cube[:, :, :, :, 0]
    else:
        layer = cube[:, :, :, :, 7]
    return layer.reshape(n, c, 64)

def halo_index(s):
    every = slice(None)
    within = slice(1, 9)
    table = [(every, every, 0, within, within), (every, every, 9, within, within), (every, every, within, 0, within), (every, every, within, 9, within), (every, every, within, within, 0), (every, every, within, within, 9)]
    return table[s]

def face_index(s):
    every = slice(None)
    table = [(every, every, 0), (every, every, 7), (every, every, every, 0), (every, every, every, 7), (every, every, every, every, 0), (every, every, every, every, 7)]
    return table[s]

def put_halo(bordered_volume, s, layer):
    n, c = (bordered_volume.shape[0], bordered_volume.shape[1])
    return bordered_volume.at[halo_index(s)].set(layer.reshape(n, c, 8, 8))

def take_halo(bordered_volume, s):
    n, c = (bordered_volume.shape[0], bordered_volume.shape[1])
    return bordered_volume[halo_index(s)].reshape(n, c, 64)

def add_face(cube, s, layer):
    n, c = (cube.shape[0], cube.shape[1])
    return cube.at[face_index(s)].add(layer.reshape(n, c, 8, 8))

def window_stack(bordered_volume):
    n, c = (bordered_volume.shape[0], bordered_volume.shape[1])
    shifted = []
    for a in range(3):
        for b in range(3):
            for d in range(3):
                shifted.append(bordered_volume[:, :, a:a + 8, b:b + 8, d:d + 8].reshape(n, c, 512))
    return jnp.concatenate(shifted, axis=1)

def convolve(bordered_volume, weight_matrix):
    return jnp.einsum('ah,thp->tap', weight_matrix, window_stack(bordered_volume), precision=lax.Precision.HIGHEST)

def reference(features, grad_out, weights, live_count, neighbor, send_list):
    devices = N_RX * N_RY
    total = features.shape[0]
    chans = features.shape[1]
    device = jnp.arange(total, dtype=jnp.int32) // B_DEV
    grid_row = device // N_RY
    grid_col = device % N_RY
    live_mask = jnp.arange(total, dtype=jnp.int32) % B_DEV < live_count[device]
    feat_live = jnp.where(live_mask[:, None, None], features, jnp.zeros_like(features))
    grad_live = jnp.where(live_mask[:, None, None], grad_out, jnp.zeros_like(grad_out))
    sources = []
    for s in range(6):
        entry_val = neighbor[:, s]
        source = jnp.where((entry_val >= 0) & (entry_val < B_DEV), device * B_DEV + entry_val, total)
        if s < 4:
            k = jnp.clip((entry_val - B_DEV) % CAP, 0, CAP - 1)
            peer_row = jnp.clip(grid_row + [-1, 1, 0, 0][s], 0, N_RX - 1)
            peer_col = jnp.clip(grid_col + [0, 0, -1, 1][s], 0, N_RY - 1)
            peer_dev = peer_row * N_RY + peer_col
            slot_index = send_list[peer_dev * 4 + (s ^ 1), k]
            remote = (entry_val >= B_DEV) & (slot_index >= 0)
            source = jnp.where(remote, peer_dev * B_DEV + slot_index, source)
        sources.append(source.astype(jnp.int32))
    source = jnp.stack(sources, axis=1)
    feat_cube = feat_live.reshape(total, chans, 8, 8, 8)
    faces = jnp.stack([face_of(feat_cube, s) for s in range(6)], axis=1)
    faces = jnp.concatenate([faces, jnp.zeros((1, 6, chans, 64), features.dtype)], axis=0)
    weight_matrix = weights.astype(jnp.float32).transpose(1, 0, 2).reshape(chans, 27 * chans)

    def one_device(inputs):
        feat_block, gradient_tile, block_src = inputs
        bordered_volume = jnp.pad(feat_block.reshape(B_DEV, chans, 8, 8, 8), ((0, 0), (0, 0), (1, 1), (1, 1), (1, 1)))
        for s in range(6):
            bordered_volume = put_halo(bordered_volume, s, faces[block_src[:, s], s ^ 1])
        output, pull_back = jax.vjp(convolve, bordered_volume.astype(jnp.float32), weight_matrix)
        grad_pad, grad_w = pull_back(gradient_tile.astype(jnp.float32))
        interior = grad_pad[:, :, 1:9, 1:9, 1:9].reshape(B_DEV, chans, 512)
        returned = jnp.stack([take_halo(grad_pad, s) for s in range(6)], axis=1)
        return (output.astype(jnp.bfloat16), interior, returned, grad_w)
    results = lax.map(one_device, (feat_live.reshape(devices, B_DEV, chans, 512), grad_live.reshape(devices, B_DEV, chans, 512), source.reshape(devices, B_DEV, 6)))
    output = results[0].reshape(total, chans, 512)
    interior = results[1].reshape(total, chans, 512)
    returned = results[2].reshape(total, 6, chans, 64)
    grad_w = lax.optimization_barrier(jnp.sum(results[3], axis=0))
    collected = jnp.zeros((total + 1, 6, chans, 64), jnp.float32)
    for s in range(6):
        collected = collected.at[source[:, s], s ^ 1].add(returned[:, s])
    grad_cube = interior.reshape(total, chans, 8, 8, 8)
    for s in range(6):
        grad_cube = add_face(grad_cube, s, collected[:total, s])
    output = jnp.where(live_mask[:, None, None], output, jnp.zeros_like(output))
    grad_features = jnp.where(live_mask[:, None, None], grad_cube.reshape(total, chans, 512), 0.0).astype(jnp.bfloat16)
    grad_weights = grad_w.reshape(chans, 27, chans).transpose(1, 0, 2) * (512.0 * total) ** (-0.5)
    return (output, grad_features, grad_weights)
```

```python
import functools

import jax
import jax.numpy as jnp
from jax import lax
from jax.experimental import pallas as pl
from jax.experimental.pallas import tpu as pltpu
from jax.sharding import PartitionSpec as P

MESH = pl.DeviceIdType.MESH
ROWS = 1024


def low_lanes(shape):
    return lax.broadcasted_iota(jnp.int32, shape, len(shape) - 1) < 64


def pack_kernel(live_ref, send_ref, feat_ref, grad_ref, t_ref, out_ref):
    slots = feat_ref.shape[0]

    def one(g, carry):
        both = jnp.concatenate([feat_ref[g], grad_ref[g]], axis=0).astype(jnp.float32)
        cells = jnp.transpose(both)
        cells = jnp.where(g < live_ref[0], cells, 0.0)
        t_ref[g] = cells.reshape(8, 8, 8, 128)
        return carry

    lax.fori_loop(0, slots, one, 0)
    for t in range(4):
        for k in range(send_ref.shape[1]):
            slot = send_ref[t, k]
            e = jnp.maximum(slot, 0)
            if t < 2:
                face = t_ref[e, 0 if t == 0 else 7]
            else:
                face = t_ref[e, :, 0 if t == 2 else 7]
            face = jnp.where(slot >= 0, face, 0.0)
            out_ref[t, k] = face.reshape(64, 128).astype(jnp.bfloat16)


def swap_kernel(n_rx, n_ry, send_ref, recv_ref, send_sem, recv_sem):
    row, col = lax.axis_index("rx"), lax.axis_index("ry")
    sides = [
        (row > 0, (row - 1, col)),
        (row < n_rx - 1, (row + 1, col)),
        (col > 0, (row, col - 1)),
        (col < n_ry - 1, (row, col + 1)),
    ]
    barrier = pltpu.get_barrier_semaphore()
    for there, peer in sides:

        @pl.when(there)
        def _():
            pl.semaphore_signal(barrier, inc=1, device_id=peer, device_id_type=MESH)

    peers = sum(jnp.where(there, 1, 0) for there, _ in sides)
    pl.semaphore_wait(barrier, peers)

    def copy(t, peer):
        return pltpu.make_async_remote_copy(
            src_ref=send_ref.at[t],
            dst_ref=recv_ref.at[t ^ 1],
            send_sem=send_sem.at[t],
            recv_sem=recv_sem.at[t ^ 1],
            device_id=peer,
            device_id_type=MESH,
        )

    def arrival(t, peer):
        return pltpu.make_async_remote_copy(
            src_ref=send_ref.at[t],
            dst_ref=recv_ref.at[t],
            send_sem=send_sem.at[t],
            recv_sem=recv_sem.at[t],
            device_id=peer,
            device_id_type=MESH,
        )

    for t, (there, peer) in enumerate(sides):

        @pl.when(there)
        def _():
            copy(t, peer).start()

        @pl.when(jnp.logical_not(there))
        def _():
            recv_ref[t] = jnp.zeros(recv_ref.shape[1:], recv_ref.dtype)

    for t, (there, peer) in enumerate(sides):

        @pl.when(there)
        def _():
            copy(t, peer).wait_send()
            arrival(t, peer).wait_recv()


def conv_kernel(
    slots, nb_ref, live_ref, t_ref, recv_ref, wf_ref, wb_ref,
    out_ref, gf_ref, dw_ref, pad, under, over, xs, acc,
):
    g = pl.program_id(0)
    cap = recv_ref.shape[1]

    @pl.when(g == 0)
    def _():
        pad[...] = jnp.zeros_like(pad)
        under[...] = jnp.zeros_like(under)
        over[...] = jnp.zeros_like(over)
        acc[...] = jnp.zeros_like(acc)

    own = t_ref[g]
    pad[1:9, 1:9] = own
    for s in range(4):
        entry = nb_ref[g, s]
        e = jnp.clip(entry, 0, slots - 1)
        k = jnp.maximum(entry - slots, 0) % cap
        layer = 7 if s % 2 == 0 else 0
        local = t_ref[e, layer] if s < 2 else t_ref[e, :, layer]
        far = recv_ref[s, k].astype(jnp.float32).reshape(8, 8, 128)
        face = jnp.where(entry >= slots, far, jnp.where(entry >= 0, local, 0.0))
        if s < 2:
            pad[9 * (s % 2), 1:9] = face
        else:
            pad[1:9, 9 * (s % 2)] = face
    for s, hold in ((4, under), (5, over)):
        entry = nb_ref[g, s]
        e = jnp.clip(entry, 0, slots - 1)
        hold[1:9, 1:9] = jnp.where(entry >= 0, t_ref[e], 0.0)

    mid = pad[...].reshape(100, 8, 128)
    level = lax.broadcasted_iota(jnp.int32, mid.shape, 1)
    low = pltpu.roll(jnp.where(level == 7, under[...].reshape(mid.shape), mid), 1, 1)
    high = pltpu.roll(jnp.where(level == 0, over[...].reshape(mid.shape), mid), 7, 1)
    mid, low, high = (v.reshape(800, 128) for v in (mid, low, high))
    first = low_lanes((800, 128))
    xs[:, 0:128] = jnp.where(first, low, pltpu.roll(mid, 64, 1)).astype(jnp.bfloat16)
    xs[:, 128:256] = high.astype(jnp.bfloat16)
    xs[:, 256:384] = jnp.where(first, pltpu.roll(low, 64, 1), mid).astype(jnp.bfloat16)

    yf = jnp.dot(xs[0:640, 0:256], wf_ref[0], preferred_element_type=jnp.float32)
    yb = jnp.dot(xs[0:640, 128:384], wb_ref[0], preferred_element_type=jnp.float32)
    for a in (1, 2):
        yf += jnp.dot(
            xs[80 * a : 80 * a + 640, 0:256], wf_ref[a], preferred_element_type=jnp.float32
        )
        yb += jnp.dot(
            xs[80 * a : 80 * a + 640, 128:384], wb_ref[a], preferred_element_type=jnp.float32
        )
    yf, yb = yf.reshape(8, 10, 8, 256), yb.reshape(8, 10, 8, 256)
    half = low_lanes((8, 8, 8, 128))
    swapped = jnp.where(half, yb[:, 1:9, :, 0:128], yf[:, 1:9, :, 0:128])
    total = jnp.where(half, yf[:, 0:8, :, 0:128], yb[:, 0:8, :, 0:128])
    total += yf[:, 2:10, :, 128:256] + yb[:, 2:10, :, 128:256]
    total = total.reshape(512, 128) + pltpu.roll(swapped.reshape(512, 128), 64, 1)
    total = jnp.where(g < live_ref[0], total, 0.0)
    flat = jnp.transpose(total).astype(jnp.bfloat16)
    out_ref[0] = flat[0:64]
    gf_ref[0] = flat[64:128]

    turned = pltpu.roll(own.reshape(512, 128), 64, 1).reshape(8, 8, 8, 128)
    zero = jnp.zeros((8, 1, 8, 128), jnp.float32)
    g0 = jnp.concatenate([turned, zero, zero], axis=1)
    g1 = jnp.concatenate([zero, own, zero], axis=1)
    g2 = jnp.concatenate([zero, zero, turned], axis=1)
    g01 = jnp.where(low_lanes(g0.shape), g0, g1)
    lhs = jnp.concatenate(
        [jnp.transpose(g01.reshape(640, 128)), jnp.transpose(g2.reshape(640, 128))[0:64]], axis=0
    ).astype(jnp.bfloat16)
    for a in range(3):
        acc[192 * a : 192 * a + 192] += jnp.dot(
            lhs, xs[80 * a : 80 * a + 640, 0:256], preferred_element_type=jnp.float32
        )

    @pl.when(g == slots - 1)
    def _():
        dw_ref[0:576] = acc[:, 0:128]
        top, rest = acc[0:288, 128:256], acc[288:576, 128:256]
        dw_ref[576:864] = jnp.where(low_lanes((288, 128)), top, pltpu.roll(rest, 64, 1))
        dw_ref[864:ROWS] = jnp.zeros((ROWS - 864, 128), jnp.float32)


def sum_kernel(
    n_rx, n_ry, scale, dw_ref, out_ref,
    src1, got1, src2, got2, part, whole, send_sem, sem1, sem2, sem3, sem4,
):
    row, col = lax.axis_index("rx"), lax.axis_index("ry")
    size = dw_ref.shape[0] // n_ry
    piece = size // n_rx
    cols = [lax.rem(col + d, n_ry) for d in range(1, n_ry)]
    rows = [lax.rem(row + d, n_rx) for d in range(1, n_rx)]
    barrier = pltpu.get_barrier_semaphore()
    for c in cols:
        pl.semaphore_signal(barrier, inc=1, device_id=(row, c), device_id_type=MESH)
    for r in rows:
        pl.semaphore_signal(barrier, inc=1, device_id=(r, col), device_id_type=MESH)
    src1[...] = dw_ref[...].reshape(n_ry, size, 128)
    pl.semaphore_wait(barrier, n_ry + n_rx - 2)

    def copy(src, dst, stage, n, sem, peer):
        return pltpu.make_async_remote_copy(
            src_ref=src, dst_ref=dst, send_sem=send_sem.at[stage, n], recv_sem=sem,
            device_id=peer, device_id_type=MESH,
        )

    sent = []
    for n, c in enumerate(cols):
        x = copy(src1.at[c], got1.at[col], 0, n, sem1.at[col], (row, c))
        x.start()
        sent.append(x)
    mine = dw_ref[pl.ds(pl.multiple_of(col * size, 8), size), :]
    for n, c in enumerate(reversed(cols)):
        copy(src1.at[c], got1.at[c], 0, n, sem1.at[c], (row, c)).wait_recv()
        mine += got1[c]

    src2[...] = mine.reshape(n_rx, piece, 128)
    for n, r in enumerate(rows):
        x = copy(src2.at[r], got2.at[row], 1, n, sem2.at[row], (r, col))
        x.start()
        sent.append(x)
    small = src2[row]
    for n, r in enumerate(reversed(rows)):
        copy(src2.at[r], got2.at[r], 1, n, sem2.at[r], (r, col)).wait_recv()
        small += got2[r]

    part[row] = (small * scale).astype(part.dtype)
    for n, r in enumerate(rows):
        x = copy(part.at[row], part.at[row], 2, n, sem3.at[row], (r, col))
        x.start()
        sent.append(x)
    for n, r in enumerate(reversed(rows)):
        copy(part.at[r], part.at[r], 2, n, sem3.at[r], (r, col)).wait_recv()

    for n, c in enumerate(cols):
        x = copy(part, whole.at[col], 3, n, sem4.at[col], (row, c))
        x.start()
        sent.append(x)
    out_ref[col] = part[...].astype(jnp.float32)
    for n, c in enumerate(reversed(cols)):
        copy(part, whole.at[c], 3, n, sem4.at[c], (row, c)).wait_recv()
        out_ref[c] = whole[c].astype(jnp.float32)
    for x in sent:
        x.wait_send()


def body(features, grad_out, weights, live_count, neighbor, send_list):
    slots, channels = features.shape[0], features.shape[1]
    cap = send_list.shape[1]
    n_rx, n_ry = lax.axis_size("rx"), lax.axis_size("ry")
    f32, bf16 = jnp.float32, jnp.bfloat16
    vmem = pl.BlockSpec(memory_space=pltpu.VMEM)
    smem = pl.BlockSpec(memory_space=pltpu.SMEM)

    cells, faces = pl.pallas_call(
        pack_kernel,
        out_shape=(
            jax.ShapeDtypeStruct((slots, 8, 8, 8, 128), f32),
            jax.ShapeDtypeStruct((4, cap, 64, 128), bf16),
        ),
        in_specs=[smem, smem, vmem, vmem],
        out_specs=(vmem, vmem),
        name="pack",
    )(live_count, send_list, features, grad_out)

    received = pl.pallas_call(
        functools.partial(swap_kernel, n_rx, n_ry),
        out_shape=jax.ShapeDtypeStruct((4, cap, 64, 128), bf16),
        in_specs=[vmem],
        out_specs=vmem,
        scratch_shapes=[pltpu.SemaphoreType.DMA((4,)), pltpu.SemaphoreType.DMA((4,))],
        compiler_params=pltpu.CompilerParams(collective_id=0, has_side_effects=True),
        name="swap",
    )(faces)

    by_offset = weights.reshape(3, 3, 3, channels, channels)
    forward = by_offset.transpose(0, 2, 4, 1, 3).reshape(3, 192, 192)
    forward = jnp.pad(forward, ((0, 0), (0, 64), (0, 64)))
    backward = by_offset[::-1, ::-1, ::-1].transpose(0, 2, 3, 1, 4)
    gap = jnp.zeros((3, 3, 64, 1, 64), bf16)
    backward = jnp.concatenate(
        [backward[:, :, :, 1:2], backward[:, :, :, 0:1], gap, backward[:, :, :, 2:3]], axis=3
    ).reshape(3, 3, 64, 256)
    backward = jnp.concatenate(
        [jnp.zeros((3, 64, 256), bf16), backward[:, 2], backward[:, 0], backward[:, 1]], axis=1
    )

    block = pl.BlockSpec((1, channels, 512), lambda g: (g, 0, 0))
    output, grad_features, dw = pl.pallas_call(
        functools.partial(conv_kernel, slots),
        grid=(slots,),
        out_shape=(
            jax.ShapeDtypeStruct(features.shape, bf16),
            jax.ShapeDtypeStruct(features.shape, bf16),
            jax.ShapeDtypeStruct((ROWS, 128), f32),
        ),
        in_specs=[smem, smem, vmem, vmem, vmem, vmem],
        out_specs=(block, block, pl.BlockSpec((ROWS, 128), lambda g: (0, 0))),
        scratch_shapes=[
            pltpu.VMEM((10, 10, 8, 128), f32),
            pltpu.VMEM((10, 10, 8, 128), f32),
            pltpu.VMEM((10, 10, 8, 128), f32),
            pltpu.VMEM((800, 384), bf16),
            pltpu.VMEM((576, 256), f32),
        ],
        name="conv",
    )(neighbor, live_count, cells, received, forward, backward)

    scale = (512.0 * slots * n_rx * n_ry) ** (-0.5)
    size = ROWS // n_ry
    piece = size // n_rx
    most = max(n_rx, n_ry)
    summed = pl.pallas_call(
        functools.partial(sum_kernel, n_rx, n_ry, scale),
        out_shape=jax.ShapeDtypeStruct((n_ry, n_rx, piece, 128), f32),
        in_specs=[vmem],
        out_specs=vmem,
        scratch_shapes=[
            pltpu.VMEM((n_ry, size, 128), f32),
            pltpu.VMEM((n_ry, size, 128), f32),
            pltpu.VMEM((n_rx, piece, 128), f32),
            pltpu.VMEM((n_rx, piece, 128), f32),
            pltpu.VMEM((n_rx, piece, 128), bf16),
            pltpu.VMEM((n_ry, n_rx, piece, 128), bf16),
            pltpu.SemaphoreType.DMA((4, most)),
            pltpu.SemaphoreType.DMA((n_ry,)),
            pltpu.SemaphoreType.DMA((n_rx,)),
            pltpu.SemaphoreType.DMA((n_rx,)),
            pltpu.SemaphoreType.DMA((n_ry,)),
        ],
        compiler_params=pltpu.CompilerParams(collective_id=1, has_side_effects=True),
        name="total",
    )(dw).reshape(ROWS, 128)
    pairs = summed[0:576].reshape(3, 3, 64, 2, 64)
    last = jnp.concatenate([summed[576:864, 0:64], summed[576:864, 64:128]], axis=0)
    joined = jnp.concatenate([pairs, last.reshape(3, 3, 64, 1, 64)], axis=3)
    grad_weights = joined.transpose(0, 1, 3, 2, 4).reshape(27, channels, channels)
    return output, grad_features, grad_weights


def solution(mesh):
    placed = (
        P(("rx", "ry"), None, None),
        P(("rx", "ry"), None, None),
        P(),
        P(("rx", "ry")),
        P(("rx", "ry"), None),
        P(("rx", "ry"), None),
    )
    return jax.shard_map(
        body,
        mesh=mesh,
        in_specs=placed,
        out_specs=(P(("rx", "ry"), None, None), P(("rx", "ry"), None, None), P()),
        check_vma=False,
    )
```

```python
import functools

import jax
import jax.numpy as jnp
from jax import lax
from jax.experimental import pallas as pl
from jax.experimental.pallas import tpu as pltpu
from jax.sharding import PartitionSpec as P

MESH = pl.DeviceIdType.MESH
ROWS = 1024


def low_lanes(shape):
    return lax.broadcasted_iota(jnp.int32, shape, len(shape) - 1) < 64


def pack_kernel(live_ref, send_ref, feat_ref, grad_ref, t_ref, out_ref):
    slots = feat_ref.shape[0]

    def one(g, carry):
        both = jnp.concatenate([feat_ref[g], grad_ref[g]], axis=0).astype(jnp.float32)
        cells = jnp.transpose(both)
        cells = jnp.where(g < live_ref[0], cells, 0.0)
        t_ref[g] = cells.reshape(8, 8, 8, 128)
        return carry

    lax.fori_loop(0, slots, one, 0)
    for t in range(4):
        for k in range(send_ref.shape[1]):
            slot = send_ref[t, k]
            e = jnp.maximum(slot, 0)
            if t < 2:
                face = t_ref[e, 0 if t == 0 else 7]
            else:
                face = t_ref[e, :, 0 if t == 2 else 7]
            face = jnp.where(slot >= 0, face, 0.0)
            out_ref[t, k] = face.reshape(64, 128).astype(jnp.bfloat16)


def swap_kernel(
    n_rx, n_ry, live_ref, list_ref, feat_ref, grad_ref, w_ref,
    t_ref, recv_ref, wf_ref, wb_ref, send_ref, send_sem, recv_sem,
):
    row, col = lax.axis_index("rx"), lax.axis_index("ry")
    sides = [
        (row > 0, (row - 1, col)),
        (row < n_rx - 1, (row + 1, col)),
        (col > 0, (row, col - 1)),
        (col < n_ry - 1, (row, col + 1)),
    ]
    barrier = pltpu.get_barrier_semaphore()
    for there, peer in sides:

        @pl.when(there)
        def _():
            pl.semaphore_signal(barrier, inc=1, device_id=peer, device_id_type=MESH)

    pack_kernel(live_ref, list_ref, feat_ref, grad_ref, t_ref, send_ref)
    peers = sum(jnp.where(there, 1, 0) for there, _ in sides)
    pl.semaphore_wait(barrier, peers)

    def copy(t, into, peer):
        return pltpu.make_async_remote_copy(
            src_ref=send_ref.at[t],
            dst_ref=recv_ref.at[into],
            send_sem=send_sem.at[t],
            recv_sem=recv_sem.at[into],
            device_id=peer,
            device_id_type=MESH,
        )

    for t, (there, peer) in enumerate(sides):

        @pl.when(there)
        def _():
            copy(t, t ^ 1, peer).start()

        @pl.when(jnp.logical_not(there))
        def _():
            recv_ref[t] = jnp.zeros(recv_ref.shape[1:], recv_ref.dtype)

    gap = jnp.zeros((64, 64), jnp.float32)
    wide = jnp.zeros((64, 256), jnp.bfloat16)
    for a in range(3):
        wf_ref[a, 192:256] = wide
        wb_ref[a, 0:64] = wide
        for c in range(3):
            ahead = [w_ref[9 * a + 3 * b + c].astype(jnp.float32) for b in range(3)]
            block = jnp.transpose(jnp.concatenate(ahead + [gap], axis=0))
            wf_ref[a, 64 * c : 64 * c + 64] = block.astype(jnp.bfloat16)
            back = [w_ref[26 - 9 * a - 3 * b - c].astype(jnp.float32) for b in range(3)]
            block = jnp.concatenate([back[1], back[0], gap, back[2]], axis=1)
            at = 64 * (2, 3, 1)[c]
            wb_ref[a, at : at + 64] = block.astype(jnp.bfloat16)

    for t, (there, peer) in enumerate(sides):

        @pl.when(there)
        def _():
            copy(t, t ^ 1, peer).wait_send()
            copy(t, t, peer).wait_recv()


def conv_kernel(
    slots, nb_ref, live_ref, t_ref, recv_ref, wf_ref, wb_ref,
    out_ref, gf_ref, dw_ref, pad, under, over, xs, acc,
):
    g = pl.program_id(0)
    cap = recv_ref.shape[1]

    @pl.when(g == 0)
    def _():
        pad[...] = jnp.zeros_like(pad)
        under[...] = jnp.zeros_like(under)
        over[...] = jnp.zeros_like(over)
        acc[...] = jnp.zeros_like(acc)

    own = t_ref[g]
    pad[1:9, 1:9] = own
    for s in range(4):
        entry = nb_ref[g, s]
        e = jnp.clip(entry, 0, slots - 1)
        k = jnp.maximum(entry - slots, 0) % cap
        layer = 7 if s % 2 == 0 else 0
        local = t_ref[e, layer] if s < 2 else t_ref[e, :, layer]
        far = recv_ref[s, k].astype(jnp.float32).reshape(8, 8, 128)
        face = jnp.where(entry >= slots, far, jnp.where(entry >= 0, local, 0.0))
        if s < 2:
            pad[9 * (s % 2), 1:9] = face
        else:
            pad[1:9, 9 * (s % 2)] = face
    for s, hold in ((4, under), (5, over)):
        entry = nb_ref[g, s]
        e = jnp.clip(entry, 0, slots - 1)
        hold[1:9, 1:9] = jnp.where(entry >= 0, t_ref[e], 0.0)

    mid = pad[...].reshape(100, 8, 128)
    level = lax.broadcasted_iota(jnp.int32, mid.shape, 1)
    low = pltpu.roll(jnp.where(level == 7, under[...].reshape(mid.shape), mid), 1, 1)
    high = pltpu.roll(jnp.where(level == 0, over[...].reshape(mid.shape), mid), 7, 1)
    mid, low, high = (v.reshape(800, 128) for v in (mid, low, high))
    first = low_lanes((800, 128))
    xs[:, 0:128] = jnp.where(first, low, pltpu.roll(mid, 64, 1)).astype(jnp.bfloat16)
    xs[:, 128:256] = high.astype(jnp.bfloat16)
    xs[:, 256:384] = jnp.where(first, pltpu.roll(low, 64, 1), mid).astype(jnp.bfloat16)

    yf = jnp.dot(xs[0:640, 0:256], wf_ref[0], preferred_element_type=jnp.float32)
    yb = jnp.dot(xs[0:640, 128:384], wb_ref[0], preferred_element_type=jnp.float32)
    for a in (1, 2):
        yf += jnp.dot(
            xs[80 * a : 80 * a + 640, 0:256], wf_ref[a], preferred_element_type=jnp.float32
        )
        yb += jnp.dot(
            xs[80 * a : 80 * a + 640, 128:384], wb_ref[a], preferred_element_type=jnp.float32
        )
    yf, yb = yf.reshape(8, 10, 8, 256), yb.reshape(8, 10, 8, 256)
    half = low_lanes((8, 8, 8, 128))
    swapped = jnp.where(half, yb[:, 1:9, :, 0:128], yf[:, 1:9, :, 0:128])
    total = jnp.where(half, yf[:, 0:8, :, 0:128], yb[:, 0:8, :, 0:128])
    total += yf[:, 2:10, :, 128:256] + yb[:, 2:10, :, 128:256]
    total = total.reshape(512, 128) + pltpu.roll(swapped.reshape(512, 128), 64, 1)
    total = jnp.where(g < live_ref[0], total, 0.0)
    flat = jnp.transpose(total).astype(jnp.bfloat16)
    out_ref[0] = flat[0:64]
    gf_ref[0] = flat[64:128]

    turned = pltpu.roll(own.reshape(512, 128), 64, 1).reshape(8, 8, 8, 128)
    zero = jnp.zeros((8, 1, 8, 128), jnp.float32)
    g0 = jnp.concatenate([turned, zero, zero], axis=1)
    g1 = jnp.concatenate([zero, own, zero], axis=1)
    g2 = jnp.concatenate([zero, zero, turned], axis=1)
    g01 = jnp.where(low_lanes(g0.shape), g0, g1)
    lhs = jnp.concatenate(
        [jnp.transpose(g01.reshape(640, 128)), jnp.transpose(g2.reshape(640, 128))[0:64]], axis=0
    ).astype(jnp.bfloat16)
    for a in range(3):
        acc[192 * a : 192 * a + 192] += jnp.dot(
            lhs, xs[80 * a : 80 * a + 640, 0:256], preferred_element_type=jnp.float32
        )

    @pl.when(g == slots - 1)
    def _():
        dw_ref[0:576] = acc[:, 0:128]
        rest = jnp.concatenate([acc[320:576, 128:256], jnp.zeros((64, 128), jnp.float32)], axis=0)
        top = acc[0:320, 128:256]
        dw_ref[576:896] = jnp.where(low_lanes((320, 128)), top, pltpu.roll(rest, 64, 1))
        dw_ref[896:ROWS] = jnp.zeros((ROWS - 896, 128), jnp.float32)


def sum_kernel(
    n_rx, n_ry, scale, dw_ref, out_ref,
    src1, got1, src2, got2, part, whole, send_sem, sem1, sem2, sem3, sem4,
):
    row, col = lax.axis_index("rx"), lax.axis_index("ry")
    size = dw_ref.shape[0] // n_ry
    piece = size // n_rx
    cols = [lax.rem(col + d, n_ry) for d in range(1, n_ry)]
    rows = [lax.rem(row + d, n_rx) for d in range(1, n_rx)]
    barrier = pltpu.get_barrier_semaphore()
    for c in cols:
        pl.semaphore_signal(barrier, inc=1, device_id=(row, c), device_id_type=MESH)
    for r in rows:
        pl.semaphore_signal(barrier, inc=1, device_id=(r, col), device_id_type=MESH)
    src1[...] = dw_ref[...].reshape(n_ry, size, 128)
    pl.semaphore_wait(barrier, n_ry + n_rx - 2)

    def copy(src, dst, stage, n, sem, peer):
        return pltpu.make_async_remote_copy(
            src_ref=src, dst_ref=dst, send_sem=send_sem.at[stage, n], recv_sem=sem,
            device_id=peer, device_id_type=MESH,
        )

    sent = []
    for n, c in enumerate(cols):
        x = copy(src1.at[c], got1.at[col], 0, n, sem1.at[col], (row, c))
        x.start()
        sent.append(x)
    mine = dw_ref[pl.ds(pl.multiple_of(col * size, 8), size), :]
    for n, c in enumerate(reversed(cols)):
        copy(src1.at[c], got1.at[c], 0, n, sem1.at[c], (row, c)).wait_recv()
        mine += got1[c]

    src2[...] = mine.reshape(n_rx, piece, 128)
    for n, r in enumerate(rows):
        x = copy(src2.at[r], got2.at[row], 1, n, sem2.at[row], (r, col))
        x.start()
        sent.append(x)
    small = src2[row]
    for n, r in enumerate(reversed(rows)):
        copy(src2.at[r], got2.at[r], 1, n, sem2.at[r], (r, col)).wait_recv()
        small += got2[r]

    part[row] = (small * scale).astype(part.dtype)
    for n, r in enumerate(rows):
        x = copy(part.at[row], part.at[row], 2, n, sem3.at[row], (r, col))
        x.start()
        sent.append(x)
    for n, r in enumerate(reversed(rows)):
        copy(part.at[r], part.at[r], 2, n, sem3.at[r], (r, col)).wait_recv()

    for n, c in enumerate(cols):
        x = copy(part, whole.at[col], 3, n, sem4.at[col], (row, c))
        x.start()
        sent.append(x)
    whole[col] = part[...]
    for n, c in enumerate(reversed(cols)):
        copy(part, whole.at[c], 3, n, sem4.at[c], (row, c)).wait_recv()
    full = whole[...].astype(jnp.float32).reshape(ROWS, 128)
    for n in range(9):
        pair = full[64 * n : 64 * n + 64]
        out_ref[3 * n] = pair[:, 0:64]
        out_ref[3 * n + 1] = pair[:, 64:128]
        at, half = 576 + 64 * (n % 5), 64 * (n // 5)
        out_ref[3 * n + 2] = full[at : at + 64, half : half + 64]
    for x in sent:
        x.wait_send()


def body(features, grad_out, weights, live_count, neighbor, send_list):
    slots, channels = features.shape[0], features.shape[1]
    cap = send_list.shape[1]
    n_rx, n_ry = lax.axis_size("rx"), lax.axis_size("ry")
    f32, bf16 = jnp.float32, jnp.bfloat16
    vmem = pl.BlockSpec(memory_space=pltpu.VMEM)
    smem = pl.BlockSpec(memory_space=pltpu.SMEM)

    cells, received, forward, backward = pl.pallas_call(
        functools.partial(swap_kernel, n_rx, n_ry),
        out_shape=(
            jax.ShapeDtypeStruct((slots, 8, 8, 8, 128), f32),
            jax.ShapeDtypeStruct((4, cap, 64, 128), bf16),
            jax.ShapeDtypeStruct((3, 256, 256), bf16),
            jax.ShapeDtypeStruct((3, 256, 256), bf16),
        ),
        in_specs=[smem, smem, vmem, vmem, vmem],
        out_specs=(vmem, vmem, vmem, vmem),
        scratch_shapes=[
            pltpu.VMEM((4, cap, 64, 128), bf16),
            pltpu.SemaphoreType.DMA((4,)),
            pltpu.SemaphoreType.DMA((4,)),
        ],
        compiler_params=pltpu.CompilerParams(collective_id=0, has_side_effects=True),
        name="swap",
    )(live_count, send_list, features, grad_out, weights)

    block = pl.BlockSpec((1, channels, 512), lambda g: (g, 0, 0))
    output, grad_features, dw = pl.pallas_call(
        functools.partial(conv_kernel, slots),
        grid=(slots,),
        out_shape=(
            jax.ShapeDtypeStruct(features.shape, bf16),
            jax.ShapeDtypeStruct(features.shape, bf16),
            jax.ShapeDtypeStruct((ROWS, 128), f32),
        ),
        in_specs=[smem, smem, vmem, vmem, vmem, vmem],
        out_specs=(block, block, pl.BlockSpec((ROWS, 128), lambda g: (0, 0))),
        scratch_shapes=[
            pltpu.VMEM((10, 10, 8, 128), f32),
            pltpu.VMEM((10, 10, 8, 128), f32),
            pltpu.VMEM((10, 10, 8, 128), f32),
            pltpu.VMEM((800, 384), bf16),
            pltpu.VMEM((576, 256), f32),
        ],
        name="conv",
    )(neighbor, live_count, cells, received, forward, backward)

    scale = (512.0 * slots * n_rx * n_ry) ** (-0.5)
    size = ROWS // n_ry
    piece = size // n_rx
    most = max(n_rx, n_ry)
    grad_weights = pl.pallas_call(
        functools.partial(sum_kernel, n_rx, n_ry, scale),
        out_shape=jax.ShapeDtypeStruct((27, channels, channels), f32),
        in_specs=[vmem],
        out_specs=vmem,
        scratch_shapes=[
            pltpu.VMEM((n_ry, size, 128), f32),
            pltpu.VMEM((n_ry, size, 128), f32),
            pltpu.VMEM((n_rx, piece, 128), f32),
            pltpu.VMEM((n_rx, piece, 128), f32),
            pltpu.VMEM((n_rx, piece, 128), bf16),
            pltpu.VMEM((n_ry, n_rx, piece, 128), bf16),
            pltpu.SemaphoreType.DMA((4, most)),
            pltpu.SemaphoreType.DMA((n_ry,)),
            pltpu.SemaphoreType.DMA((n_rx,)),
            pltpu.SemaphoreType.DMA((n_rx,)),
            pltpu.SemaphoreType.DMA((n_ry,)),
        ],
        compiler_params=pltpu.CompilerParams(collective_id=1, has_side_effects=True),
        name="total",
    )(dw)
    return output, grad_features, grad_weights


def solution(mesh):
    placed = (
        P(("rx", "ry"), None, None),
        P(("rx", "ry"), None, None),
        P(),
        P(("rx", "ry")),
        P(("rx", "ry"), None),
        P(("rx", "ry"), None),
    )
    return jax.shard_map(
        body,
        mesh=mesh,
        in_specs=placed,
        out_specs=(P(("rx", "ry"), None, None), P(("rx", "ry"), None, None), P()),
        check_vma=False,
    )
```

```python
import functools

import jax
import jax.numpy as jnp
from jax import lax
from jax.experimental import pallas as pl
from jax.experimental.pallas import tpu as pltpu
from jax.sharding import PartitionSpec as P

MESH = pl.DeviceIdType.MESH
ROWS = 1024


def low_lanes(shape):
    return lax.broadcasted_iota(jnp.int32, shape, len(shape) - 1) < 64


def pack_kernel(live_ref, send_ref, feat_ref, grad_ref, t_ref, out_ref):
    slots = feat_ref.shape[0]

    def one(g, carry):
        both = jnp.concatenate([feat_ref[g], grad_ref[g]], axis=0).astype(jnp.float32)
        cells = jnp.transpose(both)
        cells = jnp.where(g < live_ref[0], cells, 0.0)
        t_ref[g] = cells.reshape(8, 8, 8, 128)
        return carry

    lax.fori_loop(0, slots, one, 0)
    for t in range(4):
        for k in range(send_ref.shape[1]):
            slot = send_ref[t, k]
            e = jnp.maximum(slot, 0)
            if t < 2:
                face = t_ref[e, 0 if t == 0 else 7]
            else:
                face = t_ref[e, :, 0 if t == 2 else 7]
            face = jnp.where(slot >= 0, face, 0.0)
            out_ref[t, k] = face.reshape(64, 128).astype(jnp.bfloat16)


def swap_kernel(
    n_rx, n_ry, live_ref, list_ref, feat_ref, grad_ref, w_ref,
    t_ref, recv_ref, wf_ref, wb_ref, send_ref, send_sem, recv_sem,
):
    row, col = lax.axis_index("rx"), lax.axis_index("ry")
    sides = [
        (row > 0, (row - 1, col)),
        (row < n_rx - 1, (row + 1, col)),
        (col > 0, (row, col - 1)),
        (col < n_ry - 1, (row, col + 1)),
    ]
    barrier = pltpu.get_barrier_semaphore()
    for there, peer in sides:

        @pl.when(there)
        def _():
            pl.semaphore_signal(barrier, inc=1, device_id=peer, device_id_type=MESH)

    pack_kernel(live_ref, list_ref, feat_ref, grad_ref, t_ref, send_ref)
    peers = sum(jnp.where(there, 1, 0) for there, _ in sides)
    pl.semaphore_wait(barrier, peers)

    def copy(t, into, peer):
        return pltpu.make_async_remote_copy(
            src_ref=send_ref.at[t],
            dst_ref=recv_ref.at[into],
            send_sem=send_sem.at[t],
            recv_sem=recv_sem.at[into],
            device_id=peer,
            device_id_type=MESH,
        )

    for t, (there, peer) in enumerate(sides):

        @pl.when(there)
        def _():
            copy(t, t ^ 1, peer).start()

        @pl.when(jnp.logical_not(there))
        def _():
            recv_ref[t] = jnp.zeros(recv_ref.shape[1:], recv_ref.dtype)

    gap = jnp.zeros((64, 64), jnp.float32)
    wide = jnp.zeros((64, 256), jnp.bfloat16)
    for a in range(3):
        wf_ref[a, 192:256] = wide
        wb_ref[a, 0:64] = wide
        for c in range(3):
            ahead = [w_ref[9 * a + 3 * b + c].astype(jnp.float32) for b in range(3)]
            block = jnp.transpose(jnp.concatenate(ahead + [gap], axis=0))
            wf_ref[a, 64 * c : 64 * c + 64] = block.astype(jnp.bfloat16)
            back = [w_ref[26 - 9 * a - 3 * b - c].astype(jnp.float32) for b in range(3)]
            block = jnp.concatenate([back[1], back[0], gap, back[2]], axis=1)
            at = 64 * (2, 3, 1)[c]
            wb_ref[a, at : at + 64] = block.astype(jnp.bfloat16)

    for t, (there, peer) in enumerate(sides):

        @pl.when(there)
        def _():
            copy(t, t ^ 1, peer).wait_send()
            copy(t, t, peer).wait_recv()


def apply_brick(g, live_ref, xs_ref, wf_ref, wb_ref, out_ref, gf_ref):
    yf = jnp.dot(xs_ref[g, 0:640, 0:256], wf_ref[0], preferred_element_type=jnp.float32)
    yb = jnp.dot(xs_ref[g, 0:640, 128:384], wb_ref[0], preferred_element_type=jnp.float32)
    for a in (1, 2):
        yf += jnp.dot(
            xs_ref[g, 80 * a : 80 * a + 640, 0:256], wf_ref[a], preferred_element_type=jnp.float32
        )
        yb += jnp.dot(
            xs_ref[g, 80 * a : 80 * a + 640, 128:384], wb_ref[a], preferred_element_type=jnp.float32
        )
    yf, yb = yf.reshape(8, 10, 8, 256), yb.reshape(8, 10, 8, 256)
    half = low_lanes((8, 8, 8, 128))
    swapped = jnp.where(half, yb[:, 1:9, :, 0:128], yf[:, 1:9, :, 0:128])
    total = jnp.where(half, yf[:, 0:8, :, 0:128], yb[:, 0:8, :, 0:128])
    total += yf[:, 2:10, :, 128:256] + yb[:, 2:10, :, 128:256]
    total = total.reshape(512, 128) + pltpu.roll(swapped.reshape(512, 128), 64, 1)
    total = jnp.where(g < live_ref[0], total, 0.0)
    flat = jnp.transpose(total).astype(jnp.bfloat16)
    out_ref[g] = flat[0:64]
    gf_ref[g] = flat[64:128]


def conv_kernel(
    slots, nb_ref, t_ref, recv_ref, xs_ref, dw_ref, pad, under, over, acc,
):
    xs = xs_ref.at[0]
    g = pl.program_id(0)
    cap = recv_ref.shape[1]

    @pl.when(g == 0)
    def _():
        pad[...] = jnp.zeros_like(pad)
        under[...] = jnp.zeros_like(under)
        over[...] = jnp.zeros_like(over)
        acc[...] = jnp.zeros_like(acc)

    own = t_ref[g]
    pad[1:9, 1:9] = own
    for s in range(4):
        entry = nb_ref[g, s]
        e = jnp.clip(entry, 0, slots - 1)
        k = jnp.maximum(entry - slots, 0) % cap
        layer = 7 if s % 2 == 0 else 0
        local = t_ref[e, layer] if s < 2 else t_ref[e, :, layer]
        far = recv_ref[s, k].astype(jnp.float32).reshape(8, 8, 128)
        face = jnp.where(entry >= slots, far, jnp.where(entry >= 0, local, 0.0))
        if s < 2:
            pad[9 * (s % 2), 1:9] = face
        else:
            pad[1:9, 9 * (s % 2)] = face
    for s, hold in ((4, under), (5, over)):
        entry = nb_ref[g, s]
        e = jnp.clip(entry, 0, slots - 1)
        hold[1:9, 1:9] = jnp.where(entry >= 0, t_ref[e], 0.0)

    mid = pad[...].reshape(100, 8, 128)
    level = lax.broadcasted_iota(jnp.int32, mid.shape, 1)
    low = pltpu.roll(jnp.where(level == 7, under[...].reshape(mid.shape), mid), 1, 1)
    high = pltpu.roll(jnp.where(level == 0, over[...].reshape(mid.shape), mid), 7, 1)
    mid, low, high = (v.reshape(800, 128) for v in (mid, low, high))
    first = low_lanes((800, 128))
    xs[:, 0:128] = jnp.where(first, low, pltpu.roll(mid, 64, 1)).astype(jnp.bfloat16)
    xs[:, 128:256] = high.astype(jnp.bfloat16)
    xs[:, 256:384] = jnp.where(first, pltpu.roll(low, 64, 1), mid).astype(jnp.bfloat16)

    turned = pltpu.roll(own.reshape(512, 128), 64, 1).reshape(8, 8, 8, 128)
    zero = jnp.zeros((8, 1, 8, 128), jnp.float32)
    g0 = jnp.concatenate([turned, zero, zero], axis=1)
    g1 = jnp.concatenate([zero, own, zero], axis=1)
    g2 = jnp.concatenate([zero, zero, turned], axis=1)
    g01 = jnp.where(low_lanes(g0.shape), g0, g1)
    lhs = jnp.concatenate(
        [jnp.transpose(g01.reshape(640, 128)), jnp.transpose(g2.reshape(640, 128))[0:64]], axis=0
    ).astype(jnp.bfloat16)
    for a in range(3):
        acc[192 * a : 192 * a + 192] += jnp.dot(
            lhs, xs[80 * a : 80 * a + 640, 0:256], preferred_element_type=jnp.float32
        )

    @pl.when(g == slots - 1)
    def _():
        dw_ref[0:576] = acc[:, 0:128]
        rest = jnp.concatenate([acc[320:576, 128:256], jnp.zeros((64, 128), jnp.float32)], axis=0)
        top = acc[0:320, 128:256]
        dw_ref[576:896] = jnp.where(low_lanes((320, 128)), top, pltpu.roll(rest, 64, 1))
        dw_ref[896:ROWS] = jnp.zeros((ROWS - 896, 128), jnp.float32)


def sum_kernel(
    n_rx, n_ry, scale, live_ref, dw_ref, xs_ref, wf_ref, wb_ref, conv_ref, gf_ref, out_ref,
    src1, got1, src2, got2, part, whole, send_sem, sem1, sem2, sem3, sem4,
):
    slots = xs_ref.shape[0]

    def brick(g, carry=0):
        apply_brick(g, live_ref, xs_ref, wf_ref, wb_ref, conv_ref, gf_ref)
        return carry

    row, col = lax.axis_index("rx"), lax.axis_index("ry")
    size = dw_ref.shape[0] // n_ry
    piece = size // n_rx
    cols = [lax.rem(col + d, n_ry) for d in range(1, n_ry)]
    rows = [lax.rem(row + d, n_rx) for d in range(1, n_rx)]
    barrier = pltpu.get_barrier_semaphore()
    for c in cols:
        pl.semaphore_signal(barrier, inc=1, device_id=(row, c), device_id_type=MESH)
    for r in rows:
        pl.semaphore_signal(barrier, inc=1, device_id=(r, col), device_id_type=MESH)
    src1[...] = dw_ref[...].reshape(n_ry, size, 128)
    pl.semaphore_wait(barrier, n_ry + n_rx - 2)

    def copy(src, dst, stage, n, sem, peer):
        return pltpu.make_async_remote_copy(
            src_ref=src, dst_ref=dst, send_sem=send_sem.at[stage, n], recv_sem=sem,
            device_id=peer, device_id_type=MESH,
        )

    sent = []
    for n, c in enumerate(cols):
        x = copy(src1.at[c], got1.at[col], 0, n, sem1.at[col], (row, c))
        x.start()
        sent.append(x)
    lax.fori_loop(0, slots - 3, brick, 0)
    mine = dw_ref[pl.ds(pl.multiple_of(col * size, 8), size), :]
    for n, c in enumerate(reversed(cols)):
        copy(src1.at[c], got1.at[c], 0, n, sem1.at[c], (row, c)).wait_recv()
        mine += got1[c]

    src2[...] = mine.reshape(n_rx, piece, 128)
    for n, r in enumerate(rows):
        x = copy(src2.at[r], got2.at[row], 1, n, sem2.at[row], (r, col))
        x.start()
        sent.append(x)
    brick(slots - 3)
    small = src2[row]
    for n, r in enumerate(reversed(rows)):
        copy(src2.at[r], got2.at[r], 1, n, sem2.at[r], (r, col)).wait_recv()
        small += got2[r]

    part[row] = (small * scale).astype(part.dtype)
    for n, r in enumerate(rows):
        x = copy(part.at[row], part.at[row], 2, n, sem3.at[row], (r, col))
        x.start()
        sent.append(x)
    brick(slots - 2)
    for n, r in enumerate(reversed(rows)):
        copy(part.at[r], part.at[r], 2, n, sem3.at[r], (r, col)).wait_recv()

    for n, c in enumerate(cols):
        x = copy(part, whole.at[col], 3, n, sem4.at[col], (row, c))
        x.start()
        sent.append(x)
    whole[col] = part[...]
    brick(slots - 1)
    for n, c in enumerate(reversed(cols)):
        copy(part, whole.at[c], 3, n, sem4.at[c], (row, c)).wait_recv()
    full = whole[...].astype(jnp.float32).reshape(ROWS, 128)
    for n in range(9):
        pair = full[64 * n : 64 * n + 64]
        out_ref[3 * n] = pair[:, 0:64]
        out_ref[3 * n + 1] = pair[:, 64:128]
        at, half = 576 + 64 * (n % 5), 64 * (n // 5)
        out_ref[3 * n + 2] = full[at : at + 64, half : half + 64]
    for x in sent:
        x.wait_send()


def body(features, grad_out, weights, live_count, neighbor, send_list):
    slots, channels = features.shape[0], features.shape[1]
    cap = send_list.shape[1]
    n_rx, n_ry = lax.axis_size("rx"), lax.axis_size("ry")
    f32, bf16 = jnp.float32, jnp.bfloat16
    vmem = pl.BlockSpec(memory_space=pltpu.VMEM)
    smem = pl.BlockSpec(memory_space=pltpu.SMEM)

    cells, received, forward, backward = pl.pallas_call(
        functools.partial(swap_kernel, n_rx, n_ry),
        out_shape=(
            jax.ShapeDtypeStruct((slots, 8, 8, 8, 128), f32),
            jax.ShapeDtypeStruct((4, cap, 64, 128), bf16),
            jax.ShapeDtypeStruct((3, 256, 256), bf16),
            jax.ShapeDtypeStruct((3, 256, 256), bf16),
        ),
        in_specs=[smem, smem, vmem, vmem, vmem],
        out_specs=(vmem, vmem, vmem, vmem),
        scratch_shapes=[
            pltpu.VMEM((4, cap, 64, 128), bf16),
            pltpu.SemaphoreType.DMA((4,)),
            pltpu.SemaphoreType.DMA((4,)),
        ],
        compiler_params=pltpu.CompilerParams(collective_id=0, has_side_effects=True),
        name="swap",
    )(live_count, send_list, features, grad_out, weights)

    windows, dw = pl.pallas_call(
        functools.partial(conv_kernel, slots),
        grid=(slots,),
        out_shape=(
            jax.ShapeDtypeStruct((slots, 800, 384), bf16),
            jax.ShapeDtypeStruct((ROWS, 128), f32),
        ),
        in_specs=[smem, vmem, vmem],
        out_specs=(
            pl.BlockSpec((1, 800, 384), lambda g: (g, 0, 0)),
            pl.BlockSpec((ROWS, 128), lambda g: (0, 0)),
        ),
        scratch_shapes=[
            pltpu.VMEM((10, 10, 8, 128), f32),
            pltpu.VMEM((10, 10, 8, 128), f32),
            pltpu.VMEM((10, 10, 8, 128), f32),
            pltpu.VMEM((576, 256), f32),
        ],
        name="conv",
    )(neighbor, cells, received)

    scale = (512.0 * slots * n_rx * n_ry) ** (-0.5)
    size = ROWS // n_ry
    piece = size // n_rx
    most = max(n_rx, n_ry)
    output, grad_features, grad_weights = pl.pallas_call(
        functools.partial(sum_kernel, n_rx, n_ry, scale),
        out_shape=(
            jax.ShapeDtypeStruct(features.shape, bf16),
            jax.ShapeDtypeStruct(features.shape, bf16),
            jax.ShapeDtypeStruct((27, channels, channels), f32),
        ),
        in_specs=[smem, vmem, vmem, vmem, vmem],
        out_specs=(vmem, vmem, vmem),
        scratch_shapes=[
            pltpu.VMEM((n_ry, size, 128), f32),
            pltpu.VMEM((n_ry, size, 128), f32),
            pltpu.VMEM((n_rx, piece, 128), f32),
            pltpu.VMEM((n_rx, piece, 128), f32),
            pltpu.VMEM((n_rx, piece, 128), bf16),
            pltpu.VMEM((n_ry, n_rx, piece, 128), bf16),
            pltpu.SemaphoreType.DMA((4, most)),
            pltpu.SemaphoreType.DMA((n_ry,)),
            pltpu.SemaphoreType.DMA((n_rx,)),
            pltpu.SemaphoreType.DMA((n_rx,)),
            pltpu.SemaphoreType.DMA((n_ry,)),
        ],
        compiler_params=pltpu.CompilerParams(collective_id=1, has_side_effects=True),
        name="total",
    )(live_count, dw, windows, forward, backward)
    return output, grad_features, grad_weights


def solution(mesh):
    placed = (
        P(("rx", "ry"), None, None),
        P(("rx", "ry"), None, None),
        P(),
        P(("rx", "ry")),
        P(("rx", "ry"), None),
        P(("rx", "ry"), None),
    )
    return jax.shard_map(
        body,
        mesh=mesh,
        in_specs=placed,
        out_specs=(P(("rx", "ry"), None, None), P(("rx", "ry"), None, None), P()),
        check_vma=False,
    )
```

```python
import functools

import jax
import jax.numpy as jnp
from jax import lax
from jax.experimental import pallas as pl
from jax.experimental.pallas import tpu as pltpu
from jax.sharding import PartitionSpec as P

MESH = pl.DeviceIdType.MESH
ROWS = 1024


def low_lanes(shape):
    return lax.broadcasted_iota(jnp.int32, shape, len(shape) - 1) < 64


def pack_kernel(live_ref, send_ref, feat_ref, grad_ref, t_ref, out_ref):
    slots = feat_ref.shape[0]

    def one(g, carry):
        both = jnp.concatenate([feat_ref[g], grad_ref[g]], axis=0).astype(jnp.float32)
        cells = jnp.transpose(both)
        cells = jnp.where(g < live_ref[0], cells, 0.0)
        t_ref[g] = cells.reshape(8, 8, 8, 128)
        return carry

    lax.fori_loop(0, slots, one, 0)
    for t in range(4):
        for k in range(send_ref.shape[1]):
            slot = send_ref[t, k]
            e = jnp.maximum(slot, 0)
            if t < 2:
                face = t_ref[e, 0 if t == 0 else 7]
            else:
                face = t_ref[e, :, 0 if t == 2 else 7]
            face = jnp.where(slot >= 0, face, 0.0)
            out_ref[t, k] = face.reshape(64, 128).astype(jnp.bfloat16)


def swap_kernel(
    n_rx, n_ry, live_ref, list_ref, feat_ref, grad_ref, w_ref,
    t_ref, recv_ref, wf_ref, wb_ref, send_ref, send_sem, recv_sem,
):
    row, col = lax.axis_index("rx"), lax.axis_index("ry")
    sides = [
        (row > 0, (row - 1, col)),
        (row < n_rx - 1, (row + 1, col)),
        (col > 0, (row, col - 1)),
        (col < n_ry - 1, (row, col + 1)),
    ]
    barrier = pltpu.get_barrier_semaphore()
    for there, peer in sides:

        @pl.when(there)
        def _():
            pl.semaphore_signal(barrier, inc=1, device_id=peer, device_id_type=MESH)

    pack_kernel(live_ref, list_ref, feat_ref, grad_ref, t_ref, send_ref)
    peers = sum(jnp.where(there, 1, 0) for there, _ in sides)
    pl.semaphore_wait(barrier, peers)

    def copy(t, into, peer):
        return pltpu.make_async_remote_copy(
            src_ref=send_ref.at[t],
            dst_ref=recv_ref.at[into],
            send_sem=send_sem.at[t],
            recv_sem=recv_sem.at[into],
            device_id=peer,
            device_id_type=MESH,
        )

    for t, (there, peer) in enumerate(sides):

        @pl.when(there)
        def _():
            copy(t, t ^ 1, peer).start()

        @pl.when(jnp.logical_not(there))
        def _():
            recv_ref[t] = jnp.zeros(recv_ref.shape[1:], recv_ref.dtype)

    gap = jnp.zeros((64, 64), jnp.float32)
    wide = jnp.zeros((64, 256), jnp.bfloat16)
    for a in range(3):
        wf_ref[a, 192:256] = wide
        wb_ref[a, 0:64] = wide
        for c in range(3):
            ahead = [w_ref[9 * a + 3 * b + c].astype(jnp.float32) for b in range(3)]
            block = jnp.transpose(jnp.concatenate(ahead + [gap], axis=0))
            wf_ref[a, 64 * c : 64 * c + 64] = block.astype(jnp.bfloat16)
            back = [w_ref[26 - 9 * a - 3 * b - c].astype(jnp.float32) for b in range(3)]
            block = jnp.concatenate([back[1], back[0], gap, back[2]], axis=1)
            at = 64 * (2, 3, 1)[c]
            wb_ref[a, at : at + 64] = block.astype(jnp.bfloat16)

    for t, (there, peer) in enumerate(sides):

        @pl.when(there)
        def _():
            copy(t, t ^ 1, peer).wait_send()
            copy(t, t, peer).wait_recv()


def conv_kernel(
    slots, nb_ref, live_ref, t_ref, recv_ref, wf_ref, wb_ref,
    out_ref, gf_ref, dw_ref, pad, under, over, xs, acc,
):
    g = pl.program_id(0)
    cap = recv_ref.shape[1]

    @pl.when(g == 0)
    def _():
        pad[...] = jnp.zeros_like(pad)
        under[...] = jnp.zeros_like(under)
        over[...] = jnp.zeros_like(over)
        acc[...] = jnp.zeros_like(acc)

    own = t_ref[g]
    pad[1:9, 1:9] = own
    for s in range(4):
        entry = nb_ref[g, s]
        e = jnp.clip(entry, 0, slots - 1)
        k = jnp.maximum(entry - slots, 0) % cap
        layer = 7 if s % 2 == 0 else 0
        local = t_ref[e, layer] if s < 2 else t_ref[e, :, layer]
        far = recv_ref[s, k].astype(jnp.float32).reshape(8, 8, 128)
        face = jnp.where(entry >= slots, far, jnp.where(entry >= 0, local, 0.0))
        if s < 2:
            pad[9 * (s % 2), 1:9] = face
        else:
            pad[1:9, 9 * (s % 2)] = face
    for s, hold in ((4, under), (5, over)):
        entry = nb_ref[g, s]
        e = jnp.clip(entry, 0, slots - 1)
        hold[1:9, 1:9] = jnp.where(entry >= 0, t_ref[e], 0.0)

    mid = pad[...].reshape(100, 8, 128)
    level = lax.broadcasted_iota(jnp.int32, mid.shape, 1)
    low = pltpu.roll(jnp.where(level == 7, under[...].reshape(mid.shape), mid), 1, 1)
    high = pltpu.roll(jnp.where(level == 0, over[...].reshape(mid.shape), mid), 7, 1)
    mid, low, high = (v.reshape(800, 128) for v in (mid, low, high))
    first = low_lanes((800, 128))
    xs[:, 0:128] = jnp.where(first, low, pltpu.roll(mid, 64, 1)).astype(jnp.bfloat16)
    xs[:, 128:256] = high.astype(jnp.bfloat16)
    xs[:, 256:384] = jnp.where(first, pltpu.roll(low, 64, 1), mid).astype(jnp.bfloat16)

    yf = jnp.dot(xs[0:640, 0:256], wf_ref[0], preferred_element_type=jnp.float32)
    yb = jnp.dot(xs[0:640, 128:384], wb_ref[0], preferred_element_type=jnp.float32)
    for a in (1, 2):
        yf += jnp.dot(
            xs[80 * a : 80 * a + 640, 0:256], wf_ref[a], preferred_element_type=jnp.float32
        )
        yb += jnp.dot(
            xs[80 * a : 80 * a + 640, 128:384], wb_ref[a], preferred_element_type=jnp.float32
        )
    yf, yb = yf.reshape(8, 10, 8, 256), yb.reshape(8, 10, 8, 256)
    half = low_lanes((8, 8, 8, 128))
    swapped = jnp.where(half, yb[:, 1:9, :, 0:128], yf[:, 1:9, :, 0:128])
    total = jnp.where(half, yf[:, 0:8, :, 0:128], yb[:, 0:8, :, 0:128])
    total += yf[:, 2:10, :, 128:256] + yb[:, 2:10, :, 128:256]
    total = total.reshape(512, 128) + pltpu.roll(swapped.reshape(512, 128), 64, 1)
    total = jnp.where(g < live_ref[0], total, 0.0)
    flat = jnp.transpose(total).astype(jnp.bfloat16)
    out_ref[0] = flat[0:64]
    gf_ref[0] = flat[64:128]

    turned = pltpu.roll(own.reshape(512, 128), 64, 1).reshape(8, 8, 8, 128)
    zero = jnp.zeros((8, 1, 8, 128), jnp.float32)
    g0 = jnp.concatenate([turned, zero, zero], axis=1)
    g1 = jnp.concatenate([zero, own, zero], axis=1)
    g2 = jnp.concatenate([zero, zero, turned], axis=1)
    g01 = jnp.where(low_lanes(g0.shape), g0, g1)
    lhs = jnp.concatenate(
        [jnp.transpose(g01.reshape(640, 128)), jnp.transpose(g2.reshape(640, 128))[0:64]], axis=0
    ).astype(jnp.bfloat16)
    for a in range(3):
        acc[192 * a : 192 * a + 192] += jnp.dot(
            lhs, xs[80 * a : 80 * a + 640, 0:256], preferred_element_type=jnp.float32
        )

    @pl.when(g == slots - 1)
    def _():
        dw_ref[0:576] = acc[:, 0:128]
        rest = jnp.concatenate([acc[320:576, 128:256], jnp.zeros((64, 128), jnp.float32)], axis=0)
        top = acc[0:320, 128:256]
        dw_ref[576:896] = jnp.where(low_lanes((320, 128)), top, pltpu.roll(rest, 64, 1))
        dw_ref[896:ROWS] = jnp.zeros((ROWS - 896, 128), jnp.float32)


def sum_kernel(
    n_rx, n_ry, scale, dw_ref, whole,
    src1, got1, src2, got2, part, send_sem, sem1, sem2, sem3, sem4,
):
    row, col = lax.axis_index("rx"), lax.axis_index("ry")
    size = dw_ref.shape[0] // n_ry
    piece = size // n_rx
    cols = [lax.rem(col + d, n_ry) for d in range(1, n_ry)]
    rows = [lax.rem(row + d, n_rx) for d in range(1, n_rx)]
    barrier = pltpu.get_barrier_semaphore()
    for c in cols:
        pl.semaphore_signal(barrier, inc=1, device_id=(row, c), device_id_type=MESH)
    for r in rows:
        pl.semaphore_signal(barrier, inc=1, device_id=(r, col), device_id_type=MESH)
    src1[...] = dw_ref[...].reshape(n_ry, size, 128)
    pl.semaphore_wait(barrier, n_ry + n_rx - 2)

    def copy(src, dst, stage, n, sem, peer):
        return pltpu.make_async_remote_copy(
            src_ref=src, dst_ref=dst, send_sem=send_sem.at[stage, n], recv_sem=sem,
            device_id=peer, device_id_type=MESH,
        )

    sent = []
    for n, c in enumerate(cols):
        x = copy(src1.at[c], got1.at[col], 0, n, sem1.at[col], (row, c))
        x.start()
        sent.append(x)
    mine = dw_ref[pl.ds(pl.multiple_of(col * size, 8), size), :]
    for n, c in enumerate(reversed(cols)):
        copy(src1.at[c], got1.at[c], 0, n, sem1.at[c], (row, c)).wait_recv()
        mine += got1[c]

    src2[...] = mine.reshape(n_rx, piece, 128)
    for n, r in enumerate(rows):
        x = copy(src2.at[r], got2.at[row], 1, n, sem2.at[row], (r, col))
        x.start()
        sent.append(x)
    small = src2[row]
    for n, r in enumerate(reversed(rows)):
        copy(src2.at[r], got2.at[r], 1, n, sem2.at[r], (r, col)).wait_recv()
        small += got2[r]

    part[row] = (small * scale).astype(part.dtype)
    for n, r in enumerate(rows):
        x = copy(part.at[row], part.at[row], 2, n, sem3.at[row], (r, col))
        x.start()
        sent.append(x)
    for n, r in enumerate(reversed(rows)):
        copy(part.at[r], part.at[r], 2, n, sem3.at[r], (r, col)).wait_recv()

    for n, c in enumerate(cols):
        x = copy(part, whole.at[col], 3, n, sem4.at[col], (row, c))
        x.start()
        sent.append(x)
    whole[col] = part[...]
    for n, c in enumerate(reversed(cols)):
        copy(part, whole.at[c], 3, n, sem4.at[c], (row, c)).wait_recv()
    for x in sent:
        x.wait_send()


def unpack_kernel(packed_ref, out_ref):
    full = packed_ref[...].astype(jnp.float32).reshape(ROWS, 128)
    for n in range(9):
        pair = full[64 * n : 64 * n + 64]
        out_ref[3 * n] = pair[:, 0:64]
        out_ref[3 * n + 1] = pair[:, 64:128]
        at, half = 576 + 64 * (n % 5), 64 * (n // 5)
        out_ref[3 * n + 2] = full[at : at + 64, half : half + 64]


def body(features, grad_out, weights, live_count, neighbor, send_list):
    slots, channels = features.shape[0], features.shape[1]
    cap = send_list.shape[1]
    n_rx, n_ry = lax.axis_size("rx"), lax.axis_size("ry")
    f32, bf16 = jnp.float32, jnp.bfloat16
    vmem = pl.BlockSpec(memory_space=pltpu.VMEM)
    smem = pl.BlockSpec(memory_space=pltpu.SMEM)

    cells, received, forward, backward = pl.pallas_call(
        functools.partial(swap_kernel, n_rx, n_ry),
        out_shape=(
            jax.ShapeDtypeStruct((slots, 8, 8, 8, 128), f32),
            jax.ShapeDtypeStruct((4, cap, 64, 128), bf16),
            jax.ShapeDtypeStruct((3, 256, 256), bf16),
            jax.ShapeDtypeStruct((3, 256, 256), bf16),
        ),
        in_specs=[smem, smem, vmem, vmem, vmem],
        out_specs=(vmem, vmem, vmem, vmem),
        scratch_shapes=[
            pltpu.VMEM((4, cap, 64, 128), bf16),
            pltpu.SemaphoreType.DMA((4,)),
            pltpu.SemaphoreType.DMA((4,)),
        ],
        compiler_params=pltpu.CompilerParams(collective_id=0, has_side_effects=True),
        name="swap",
    )(live_count, send_list, features, grad_out, weights)

    block = pl.BlockSpec((1, channels, 512), lambda g: (g, 0, 0))
    output, grad_features, dw = pl.pallas_call(
        functools.partial(conv_kernel, slots),
        grid=(slots,),
        out_shape=(
            jax.ShapeDtypeStruct(features.shape, bf16),
            jax.ShapeDtypeStruct(features.shape, bf16),
            jax.ShapeDtypeStruct((ROWS, 128), f32),
        ),
        in_specs=[smem, smem, vmem, vmem, vmem, vmem],
        out_specs=(block, block, pl.BlockSpec((ROWS, 128), lambda g: (0, 0))),
        scratch_shapes=[
            pltpu.VMEM((10, 10, 8, 128), f32),
            pltpu.VMEM((10, 10, 8, 128), f32),
            pltpu.VMEM((10, 10, 8, 128), f32),
            pltpu.VMEM((800, 384), bf16),
            pltpu.VMEM((576, 256), f32),
        ],
        name="conv",
    )(neighbor, live_count, cells, received, forward, backward)

    scale = (512.0 * slots * n_rx * n_ry) ** (-0.5)
    size = ROWS // n_ry
    piece = size // n_rx
    most = max(n_rx, n_ry)
    packed = pl.pallas_call(
        functools.partial(sum_kernel, n_rx, n_ry, scale),
        out_shape=jax.ShapeDtypeStruct((n_ry, n_rx, piece, 128), bf16),
        in_specs=[vmem],
        out_specs=vmem,
        scratch_shapes=[
            pltpu.VMEM((n_ry, size, 128), f32),
            pltpu.VMEM((n_ry, size, 128), f32),
            pltpu.VMEM((n_rx, piece, 128), f32),
            pltpu.VMEM((n_rx, piece, 128), f32),
            pltpu.VMEM((n_rx, piece, 128), bf16),
            pltpu.SemaphoreType.DMA((4, most)),
            pltpu.SemaphoreType.DMA((n_ry,)),
            pltpu.SemaphoreType.DMA((n_rx,)),
            pltpu.SemaphoreType.DMA((n_rx,)),
            pltpu.SemaphoreType.DMA((n_ry,)),
        ],
        compiler_params=pltpu.CompilerParams(collective_id=1, has_side_effects=True),
        name="total",
    )(dw)
    grad_weights = pl.pallas_call(
        unpack_kernel,
        out_shape=jax.ShapeDtypeStruct((27, channels, channels), f32),
        in_specs=[vmem],
        out_specs=vmem,
        name="unpack",
    )(packed)
    return output, grad_features, grad_weights


def solution(mesh):
    placed = (
        P(("rx", "ry"), None, None),
        P(("rx", "ry"), None, None),
        P(),
        P(("rx", "ry")),
        P(("rx", "ry"), None),
        P(("rx", "ry"), None),
    )
    return jax.shard_map(
        body,
        mesh=mesh,
        in_specs=placed,
        out_specs=(P(("rx", "ry"), None, None), P(("rx", "ry"), None, None), P()),
        check_vma=False,
    )
```
